32 devices in a mesh: groups: 2 (over y), ctx: 4 (over z), tp: 4 (over x, core).
Axes of the slice: x: 2, y: 2, z: 4, core: 2. Of those that a mesh axis runs over, the one named last changes fastest.
Arguments:
- x_input: bfloat16 [4096, 4096], P(('groups', 'ctx', 'tp')), parts along dimension 0, may hold values from -6 to 6
- bc_input: bfloat16 [4096, 2, 1024], P(('groups', 'ctx', 'tp')), parts along dimension 0, may hold values from -6 to 6
- z_input: bfloat16 [4096, 4096], P(('groups', 'ctx', 'tp')), parts along dimension 0, may hold values from -100 to 100, as said below
- dt_input: bfloat16 [4096, 64], P(('groups', 'ctx', 'tp')), parts along dimension 0, may hold values from -1.5 to 0.5
- x_kernel: float32 [4, 4096], replicated, may hold values from -2.5 to 2.5
- x_bias: float32 [4096], replicated, may hold values from -3 to 3
- bc_kernel: float32 [4, 2, 1024], replicated, may hold values from -2.5 to 2.5
- bc_bias: float32 [2, 1024], replicated, may hold values from -3 to 3
- dt_bias: float32 [64], P('tp'), may hold values from -1 to 1
- a_log: float32 [64], P('tp'), as said below
- d_skip: float32 [64], P('tp'), may hold values from 0.5 to 2
- norm_gain: float32 [4096], P('tp'), may hold values from 0.5 to 1.5
Outputs:
- gated_out: bfloat16 [4096, 4096], P(('groups', 'ctx'), 'tp'), parts along dimension 0
The draws below stay inside these ranges and needn't reach their ends.
There are 2 independent parts, one for each index of `groups`. The reference program is written for one: setup_inputs(seed, part) draws one part's arguments, and reference() takes and returns one part's arrays. A program takes and returns all parts, laid end to end along the dimension named above; an argument that names none is the same for every part. Nothing has to cross between parts.
Inputs may be any that keep to these rules, and one draw needn't show every extreme that they name: Every entry of z_input is a product of a random sign and magnitude with a token factor and a head factor. Each head's rate exp(a_log) lies between 0.2 / 2048 and 0.1.
All inputs are finite; a program needn't handle non-finite values.
Results may differ from the reference program's by a relative error of at most 0.0034.
Values may be sent and summed in bfloat16 or wider, within the bound.
No kernel may reach another device: no remote copies, remote signals or barrier semaphores. Data moves between devices by JAX's collectives and lax.ppermute only.
A program may use at most 64 MiB of HBM per device.

```python
import jax
import jax.numpy as jnp
from jax import lax

HEADS = 64
HEAD_DIM = 64
STATE_DIM = 128
GROUPS = 8
CONV_TAPS = 4
BLOCK_LEN = 256
SEQ_LEN = 2048


def draw_z_input(key, part):
    key_rows, key_heads, key_base = jax.random.split(key, 3)
    token_scale = jnp.exp(jax.random.uniform(key_rows, (SEQ_LEN, 1), jnp.float32, jnp.log(0.5), jnp.log(5.0)))
    head_scale = jnp.exp(jax.random.uniform(key_heads, (1, HEADS), jnp.float32, jnp.log(0.5), jnp.log(5.0)))
    column_scale = jnp.repeat(head_scale, HEAD_DIM, axis=1)
    base_values = jnp.clip(jax.random.normal(key_base, (SEQ_LEN, HEADS * HEAD_DIM), jnp.float32), -4.0, 4.0)
    return (base_values * token_scale * column_scale).astype(jnp.bfloat16)


def draw_a_log(key, part):
    key_kind, key_fast, key_slow = jax.random.split(key, 3)
    fast_share = 0.5
    is_fast = jax.random.uniform(key_kind, (HEADS,), jnp.float32) < fast_share
    fast_rate = jnp.exp(jax.random.uniform(key_fast, (HEADS,), jnp.float32, jnp.log(0.04), jnp.log(0.1)))
    slow_rate = jnp.exp(jax.random.uniform(key_slow, (HEADS,), jnp.float32, jnp.log(0.2), jnp.log(0.5))) / SEQ_LEN
    return jnp.log(jnp.where(is_fast, fast_rate, slow_rate)).astype(jnp.float32)


def steps_of(rng, shape, pieces, least, top_value):
    level = 1.0
    for position, parts in pieces:
        steps = jax.random.uniform(jax.random.fold_in(jax.random.fold_in(rng, 6), position), (parts,), jnp.float32, least / len(pieces), top_value / len(pieces))
        level = level * jnp.repeat(jnp.exp(steps), shape[position] // parts).reshape((-1,) + (1,) * (len(shape) - 1 - position))
    return level


def normal_values(own_key, shape, deviation, reach, pieces=(), kind=jnp.bfloat16):
    entries = deviation * jax.random.normal(own_key, shape, jnp.float32)
    if pieces:
        entries = entries * steps_of(own_key, shape, pieces, -0.22, 0.18)
    return jnp.clip(entries, -reach, reach).astype(kind)


def setup_inputs(seed: int = 0, part: int = 0) -> dict:
    seeds = jax.random.split(jax.random.key(seed), 13)
    part_splits = jax.random.split(jax.random.fold_in(seeds[12], part), 13)
    x_input = normal_values(part_splits[0], (SEQ_LEN, HEADS * HEAD_DIM), 1.0, 6.0, ((0, 16),))
    bc_input = normal_values(part_splits[1], (SEQ_LEN, 2, GROUPS * STATE_DIM), 1.0, 6.0, ((0, 16),))
    z_input = draw_z_input(jax.random.fold_in(jax.random.fold_in(seeds[12], part), 71), part)
    dt_input = jnp.clip(-1.5 + 2.0 * jax.random.uniform(part_splits[3], (SEQ_LEN, HEADS), jnp.float32) ** steps_of(part_splits[3], (SEQ_LEN, HEADS), ((0, 16),), -0.2, 0.2), -1.5, 0.5).astype(jnp.bfloat16)
    x_kernel = normal_values(seeds[4], (CONV_TAPS, HEADS * HEAD_DIM), 0.5, 2.5, (), jnp.float32)
    x_bias = normal_values(seeds[5], (HEADS * HEAD_DIM,), 0.5, 3.0, (), jnp.float32)
    bc_kernel = normal_values(seeds[6], (CONV_TAPS, 2, GROUPS * STATE_DIM), 0.5, 2.5, (), jnp.float32)
    bc_bias = normal_values(seeds[7], (2, GROUPS * STATE_DIM), 0.5, 3.0, (), jnp.float32)
    dt_bias = jnp.clip(jax.random.uniform(seeds[8], (HEADS,), jnp.float32, -1.0, 1.0) * steps_of(seeds[8], (HEADS,), ((0, 4),), -0.4, 0.0), -1.0, 1.0)
    a_log = draw_a_log(jax.random.fold_in(seeds[12], 71), part)
    d_skip = jnp.clip(0.5 + 1.5 * jax.random.uniform(seeds[10], (HEADS,), jnp.float32) ** steps_of(seeds[10], (HEADS,), ((0, 4),), -0.2, 0.2), 0.5, 2.0)
    norm_gain = jnp.clip(1.0 + 0.1 * jax.random.normal(seeds[11], (HEADS * HEAD_DIM,), jnp.float32), 0.5, 1.5)
    return dict(x_input=x_input, bc_input=bc_input, z_input=z_input, dt_input=dt_input, x_kernel=x_kernel, x_bias=x_bias, bc_kernel=bc_kernel, bc_bias=bc_bias, dt_bias=dt_bias, a_log=a_log, d_skip=d_skip, norm_gain=norm_gain)


def conv_silu(raw_rows, kernel_taps, kernel_bias):
    seq_total = raw_rows.shape[0]
    padded = jnp.concatenate([jnp.zeros((CONV_TAPS - 1,) + raw_rows.shape[1:], jnp.float32), raw_rows.astype(jnp.float32)], axis=0)
    summed = kernel_bias + jnp.zeros(padded[:seq_total].shape, jnp.float32)
    for offset in range(CONV_TAPS):
        summed = summed + kernel_taps[offset] * padded[offset:offset + seq_total]
    return jax.nn.silu(summed).astype(jnp.bfloat16)

def reference(x_input, bc_input, z_input, dt_input, x_kernel, x_bias, bc_kernel, bc_bias, dt_bias, a_log, d_skip, norm_gain):
    per_group = HEADS // GROUPS
    x_conv = conv_silu(x_input, x_kernel, x_bias).reshape(SEQ_LEN, HEADS, HEAD_DIM)
    bc_conv = conv_silu(bc_input, bc_kernel, bc_bias).reshape(SEQ_LEN, 2, GROUPS, STATE_DIM)
    step_size = jax.nn.softplus(dt_input.astype(jnp.float32) + dt_bias)
    log_decay = step_size * -jnp.exp(a_log)
    block_count = SEQ_LEN // BLOCK_LEN
    block_items = (x_conv.reshape(block_count, BLOCK_LEN, HEADS, HEAD_DIM), bc_conv.reshape(block_count, BLOCK_LEN, 2, GROUPS, STATE_DIM), step_size.reshape(block_count, BLOCK_LEN, HEADS), log_decay.reshape(block_count, BLOCK_LEN, HEADS))
    positions = jnp.arange(BLOCK_LEN)
    causal = positions[:, None] >= positions[None, :]

    def per_block(carried, items):
        x_block, bc_block, step_block, log_block = items
        x_float = x_block.astype(jnp.float32)
        b_float = bc_block[:, 0].astype(jnp.float32)
        c_float = bc_block[:, 1].astype(jnp.float32)
        decay_sums = jnp.cumsum(log_block, axis=0)
        score_groups = jnp.einsum('tgn,sgn->gts', c_float, b_float)
        score_heads = jnp.repeat(score_groups, per_group, axis=0)
        decay_cols = decay_sums.T
        gaps = decay_cols[:, :, None] - decay_cols[:, None, :]
        decays = jnp.where(causal[None], jnp.exp(jnp.where(causal[None], gaps, 0.0)), 0.0)
        weights = (score_heads * decays * step_block.T[:, None, :]).astype(jnp.bfloat16)
        intra_out = jnp.einsum('hts,shp->thp', weights.astype(jnp.float32), x_float)
        c_heads = jnp.repeat(c_float, per_group, axis=1)
        b_heads = jnp.repeat(b_float, per_group, axis=1)
        inter_out = jnp.exp(decay_sums)[:, :, None] * jnp.einsum('thn,hpn->thp', c_heads, carried, precision=lax.Precision.HIGHEST)
        tail_scale = jnp.exp(decay_sums[-1][None, :] - decay_sums) * step_block
        scaled_x = (tail_scale[:, :, None] * x_float).astype(jnp.bfloat16)
        contrib_state = jnp.einsum('shp,shn->hpn', scaled_x.astype(jnp.float32), b_heads)
        next_state = jnp.exp(decay_sums[-1])[:, None, None] * carried + contrib_state
        block_out = intra_out + inter_out + d_skip[None, :, None] * x_float
        return (next_state, block_out)
    initial = jnp.zeros((HEADS, HEAD_DIM, STATE_DIM), jnp.float32)
    final_state, outputs = lax.scan(per_block, initial, block_items)
    ssm_out = outputs.reshape(SEQ_LEN, HEADS * HEAD_DIM)
    gated = ssm_out * jax.nn.silu(z_input.astype(jnp.float32))
    grouped = gated.reshape(SEQ_LEN, GROUPS, -1)
    mean_square = lax.optimization_barrier(jnp.mean(grouped * grouped, axis=-1, keepdims=True))
    normed = (grouped * lax.rsqrt(mean_square + 1e-05)).reshape(SEQ_LEN, HEADS * HEAD_DIM) * norm_gain
    return normed.astype(jnp.bfloat16)
```

```python
import functools

import jax
import jax.numpy as jnp
from jax import lax
from jax.experimental import pallas as pl
from jax.experimental.pallas import tpu as pltpu
from jax.sharding import PartitionSpec as P

HEADS = 64
HEAD_DIM = 64
STATE_DIM = 128
GROUPS = 8
CONV_TAPS = 4
PER_GROUP = HEADS // GROUPS
GROUP_WIDTH = PER_GROUP * HEAD_DIM
LANES = 128
X_TILES = GROUP_WIDTH // LANES
SPAN = 512
RIM = 4
EXTRA = 16
F32 = jnp.float32
BF16 = jnp.bfloat16


def partner(place, slot):
    return place ^ slot


def swap(value, slot):
    return lax.ppermute(value, "tp", [(i, i ^ slot) for i in range(lax.axis_size("tp"))])


def from_behind(value, axis, steps):
    count = lax.axis_size(axis)
    return lax.ppermute(value, axis, [(i, i + steps) for i in range(count - steps)])


def in_three(value):
    high = value.astype(BF16).astype(F32)
    rest = value - high
    middle = rest.astype(BF16).astype(F32)
    low = rest - middle
    return jnp.concatenate([high, middle, low, jnp.zeros_like(value)], axis=0).astype(BF16)


def head_columns():
    rows = lax.broadcasted_iota(jnp.int32, (4 * PER_GROUP, GROUP_WIDTH), 0)
    columns = lax.broadcasted_iota(jnp.int32, (4 * PER_GROUP, GROUP_WIDTH), 1)
    own = lax.rem(rows, PER_GROUP) == lax.div(columns, HEAD_DIM)
    return jnp.where(own, 1.0, 0.0).astype(BF16)


def spread(value, columns):
    return lax.dot_general(
        in_three(value), columns, (((0,), (0,)), ((), ())), preferred_element_type=F32
    )


def column_of(ref, first, width=LANES):
    rows = lax.broadcasted_iota(jnp.int32, (PER_GROUP, width), 0)
    out = jnp.zeros((PER_GROUP, width), F32)
    for head in range(PER_GROUP):
        out = jnp.where(rows == head, ref[first + head], out)
    return out


def conv_tile(scratch, rim, rows, taps, shift):
    count = rows.shape[0]
    scratch[8 - RIM : 8, :] = rim.astype(F32)
    scratch[8 : 8 + count, :] = rows.astype(F32)
    total = shift + jnp.zeros((count, LANES), F32)
    for tap in range(CONV_TAPS):
        first = 8 - (CONV_TAPS - 1) + tap
        total = total + taps[tap : tap + 1, :] * scratch[first : first + count, :]
    return (total / (1.0 + jnp.exp(-total))).astype(BF16)


def send_kernel(group, tp, gd, x_ref, b_ref, dt_ref, rim_ref, tx_ref, sx_ref, tb_ref, sb_ref, *rest):
    outs, scratch = rest[:tp], rest[tp]
    rows = x_ref.shape[0]
    me = lax.axis_index("tp")
    eye_r = lax.broadcasted_iota(jnp.int32, (rows, rows), 0)
    eye_c = lax.broadcasted_iota(jnp.int32, (rows, rows), 1)
    eye = jnp.where(eye_r == eye_c, 1.0, 0.0).astype(BF16)
    steps = lax.dot_general(
        dt_ref[...], eye, (((0,), (0,)), ((), ())), preferred_element_type=F32
    )
    dt_scr = rest[tp + 1]
    dt_scr[...] = steps
    for slot in range(tp):
        out = outs[slot]
        whole = partner(me, slot) * gd + group
        for tile in range(X_TILES):
            at = pl.ds(pl.multiple_of(whole * GROUP_WIDTH + tile * LANES, LANES), LANES)
            out[tile * rows : (tile + 1) * rows, :] = conv_tile(
                scratch, rim_ref[:, at], x_ref[:, at], tx_ref[:, at], sx_ref[:, at]
            )
        at = pl.ds(pl.multiple_of(whole * STATE_DIM, LANES), LANES)
        width = x_ref.shape[1]
        rim_at = pl.ds(pl.multiple_of(width + whole * STATE_DIM, LANES), LANES)
        out[X_TILES * rows : (X_TILES + 1) * rows, :] = conv_tile(
            scratch, rim_ref[:, rim_at], b_ref[:, at], tb_ref[:, at], sb_ref[:, at]
        )
        mine = dt_scr[pl.ds(pl.multiple_of(whole * PER_GROUP, PER_GROUP), PER_GROUP), :]
        out[(X_TILES + 1) * rows :, :] = jnp.concatenate(
            [mine, jnp.zeros((EXTRA - PER_GROUP, rows), F32)], axis=0
        ).astype(BF16)


def last_send_kernel(tp, gd, kept, z_ref, c_ref, rim_ref, tc_ref, sc_ref, *rest):
    outs, scratch = rest[:tp], rest[tp]
    me = lax.axis_index("tp")
    gate_width = (gd - kept) * GROUP_WIDTH
    for slot in range(tp):
        out = outs[slot]
        place = partner(me, slot)
        at = pl.ds(
            pl.multiple_of(place * (gd * GROUP_WIDTH) + kept * GROUP_WIDTH, LANES), gate_width
        )
        out[:, :gate_width] = z_ref[:, at]
        for group in range(gd):
            first = (place * gd + group) * STATE_DIM
            at = pl.ds(pl.multiple_of(first, LANES), LANES)
            rim_at = pl.ds(
                pl.multiple_of(rim_ref.shape[1] - c_ref.shape[1] + first, LANES), LANES
            )
            out[:, gate_width + group * LANES : gate_width + (group + 1) * LANES] = conv_tile(
                scratch, rim_ref[:, rim_at], c_ref[:, at], tc_ref[:, at], sc_ref[:, at]
            )


def state_kernel(group, tp, spans, bias_ref, log_ref, *rest):
    pieces = rest[:tp]
    conv_ref, scaled_ref, b_ref, grow_ref, mid_ref, prior_ref, ship_ref = rest[tp : tp + 7]
    ahead_ref = rest[tp + 7] if spans > 1 else None
    step_scr = rest[-1]
    rows = conv_ref.shape[0] // tp
    per_span = tp // spans
    me = lax.axis_index("tp")
    for slot in range(tp):
        place = partner(me, slot)
        at = pl.ds(pl.multiple_of(place * rows, rows), rows)
        for tile in range(X_TILES):
            conv_ref[at, tile * LANES : (tile + 1) * LANES] = pieces[slot][
                tile * rows : (tile + 1) * rows, :
            ]
        b_ref[at, :] = pieces[slot][X_TILES * rows : (X_TILES + 1) * rows, :]
        step_scr[place] = pieces[slot][(X_TILES + 1) * rows :, :].astype(F32)[:PER_GROUP]
    bias = column_of(bias_ref, group * PER_GROUP, rows)
    rate = jnp.exp(column_of(log_ref, group * PER_GROUP, rows))
    steps, logs = [], []
    for place in range(tp):
        raw = step_scr[place] + bias
        step = jnp.maximum(raw, 0.0) + jnp.log1p(jnp.exp(-jnp.abs(raw)))
        steps.append(step)
        logs.append(-step * rate)
    tri_r = lax.broadcasted_iota(jnp.int32, (rows, rows), 0)
    tri_c = lax.broadcasted_iota(jnp.int32, (rows, rows), 1)
    tri = jnp.where(tri_r <= tri_c, 1.0, 0.0).astype(BF16)
    parts = jnp.dot(in_three(jnp.concatenate(logs, axis=0)), tri, preferred_element_type=F32)
    count = tp * PER_GROUP
    sums = parts[:count] + parts[count : 2 * count] + parts[2 * count : 3 * count]
    columns = head_columns()
    prior = jnp.zeros((PER_GROUP, rows), F32)
    total = None
    for span in range(spans):
        inside, running = [], jnp.zeros((PER_GROUP, rows), F32)
        for piece in range(per_span):
            first = (span * per_span + piece) * PER_GROUP
            local = sums[first : first + PER_GROUP]
            inside.append(running + local)
            running = running + jnp.broadcast_to(local[:, rows - 1 :], (PER_GROUP, rows))
            if piece == max(per_span // 2 - 1, 0):
                middle = running
        for piece in range(per_span):
            place = span * per_span + piece
            grow_ref[place] = jnp.exp(inside[piece] - middle)
            scale = spread(jnp.exp(middle - inside[piece]) * steps[place], columns)
            at = slice(place * rows, (place + 1) * rows)
            scaled_ref[at, :] = (conv_ref[at, :].astype(F32) * scale).astype(BF16)
        at = slice(span * per_span * rows, (span + 1) * per_span * rows)
        summed = lax.dot_general(
            b_ref[at, :], scaled_ref[at, :], (((0,), (0,)), ((), ())), preferred_element_type=F32
        )
        summed = summed * spread(jnp.exp(running - middle), columns)
        mid_ref[span] = middle
        prior_ref[span] = prior
        if spans > 1:
            ahead_ref[span] = total if total is not None else jnp.zeros_like(summed)
        total = summed if total is None else total * spread(jnp.exp(running), columns) + summed
        prior = prior + running
    ship_ref[:STATE_DIM, :] = total.astype(BF16)
    decay = spread(jnp.exp(prior), columns)[:EXTRA]
    high = decay.astype(BF16).astype(F32)
    middle = (decay - high).astype(BF16).astype(F32)
    at = lax.broadcasted_iota(jnp.int32, (EXTRA, GROUP_WIDTH), 0)
    stacked = jnp.where(at == 0, high, jnp.where(at == 1, middle, decay - high - middle))
    ship_ref[STATE_DIM:, :] = jnp.where(at < 3, stacked, 0.0).astype(BF16)


def shipped(ref):
    rows = ref[STATE_DIM:, :].astype(F32)
    return ref[:STATE_DIM, :].astype(F32), rows[0:1] + rows[1:2] + rows[2:3]


def out_kernel(group, tp, gd, kept, spans, states, skip_ref, gain_ref, *rest):
    early, late = rest[:tp], rest[tp : 2 * tp]
    rest = rest[2 * tp :]
    conv_ref, scaled_ref, b_ref, grow_ref, mid_ref, prior_ref = rest[:6]
    rest = rest[6:]
    ahead_ref = None
    if spans > 1:
        ahead_ref, rest = rest[0], rest[1:]
    sent, rest = rest[:states], rest[states:]
    if group > 0:
        rest = rest[1:]
    out_ref, start_scr = rest
    rows = late[0].shape[0]
    span_rows = tp // spans * rows
    me = lax.axis_index("tp")
    columns = head_columns()
    state = None
    for ref in reversed(sent):
        value, decay = shipped(ref)
        state = value if state is None else state * decay + value
    for span in range(spans):
        if spans == 1:
            start_scr[span] = (state * spread(jnp.exp(mid_ref[0]), columns)).astype(BF16)
        else:
            scale = spread(jnp.exp(prior_ref[span]), columns)
            start = state * scale + ahead_ref[span]
            start_scr[span] = (start * spread(jnp.exp(mid_ref[span]), columns)).astype(BF16)
    skip = spread(column_of(skip_ref, group * PER_GROUP), columns)[:1]
    gate_width = (gd - kept) * GROUP_WIDTH
    for slot in range(tp):
        place = partner(me, slot)
        span = lax.div(place, tp // spans)
        inside = pl.ds(pl.multiple_of(span * span_rows, span_rows), span_rows)
        at = pl.ds(pl.multiple_of(place * rows, rows), rows)
        c_tile = late[slot][:, gate_width + group * LANES : gate_width + (group + 1) * LANES]
        scores = lax.dot_general(
            c_tile, b_ref[inside, :], (((1,), (1,)), ((), ())), preferred_element_type=F32
        )
        t_at = lax.broadcasted_iota(jnp.int32, scores.shape, 0) + (place * rows - span * span_rows)
        s_at = lax.broadcasted_iota(jnp.int32, scores.shape, 1)
        masked = jnp.where(s_at <= t_at, scores, 0.0).astype(BF16)
        mixed = jnp.dot(masked, scaled_ref[inside, :], preferred_element_type=F32)
        mixed = mixed + jnp.dot(c_tile, start_scr[span], preferred_element_type=F32)
        mixed = mixed * spread(grow_ref[place], columns)
        mixed = mixed + skip * conv_ref[at, :].astype(F32)
        if group < kept:
            gate = early[slot][:, group * GROUP_WIDTH : (group + 1) * GROUP_WIDTH]
        else:
            first = (group - kept) * GROUP_WIDTH
            gate = late[slot][:, first : first + GROUP_WIDTH]
        gate = gate.astype(F32)
        gated = mixed * (gate / (1.0 + jnp.exp(-gate)))
        square = jnp.mean(gated * gated, axis=-1, keepdims=True)
        out_ref[at, :] = (gated * lax.rsqrt(square + 1e-5) * gain_ref[...]).astype(BF16)


def vmem(count):
    return [pl.BlockSpec(memory_space=pltpu.VMEM)] * count


def smem(count):
    return [pl.BlockSpec(memory_space=pltpu.SMEM)] * count


def call(kernel, ins, outs, scratch, scalars=0, name=None):
    return pl.pallas_call(
        kernel,
        in_specs=smem(scalars) + vmem(len(ins) - scalars),
        out_specs=vmem(len(outs)),
        out_shape=outs,
        scratch_shapes=scratch,
        name=name,
    )(*ins)


def scanned(ship):
    count = lax.axis_size("ctx")
    if count <= 4:
        return [from_behind(ship, "ctx", steps) for steps in range(1, count)]
    state = ship[:STATE_DIM].astype(F32)
    decay = jnp.sum(ship[STATE_DIM : STATE_DIM + 3].astype(F32), axis=0, keepdims=True)

    def packed(state, decay):
        high = decay.astype(BF16).astype(F32)
        middle = (decay - high).astype(BF16).astype(F32)
        rows = [state, high, middle, decay - high - middle]
        rows.append(jnp.zeros((EXTRA - 3, GROUP_WIDTH), F32))
        return jnp.concatenate(rows, axis=0).astype(BF16)

    steps = 1
    while steps < count:
        other = from_behind(packed(state, decay), "ctx", steps)
        state = other[:STATE_DIM].astype(F32) * decay + state
        decay = decay * jnp.sum(
            other[STATE_DIM : STATE_DIM + 3].astype(F32), axis=0, keepdims=True
        )
        steps *= 2
    return [from_behind(packed(state, decay), "ctx", 1)]


def shards(
    x_input, bc_input, z_input, dt_input, x_kernel, x_bias, bc_kernel, bc_bias, dt_bias, a_log,
    d_skip, norm_gain,
):
    tp = lax.axis_size("tp")
    me = lax.axis_index("tp")
    rows = x_input.shape[0]
    ctx_rows = rows * tp
    gd = GROUPS // tp
    spans = max(1, ctx_rows // SPAN)
    kept = gd // 2
    width = gd * GROUP_WIDTH
    shape = jax.ShapeDtypeStruct

    def trade(parts):
        return [parts[0]] + [swap(parts[slot], slot) for slot in range(1, tp)]

    early = []
    if kept:
        early = trade(
            [
                lax.dynamic_slice_in_dim(
                    z_input, partner(me, slot) * width, kept * GROUP_WIDTH, 1
                )
                for slot in range(tp)
            ]
        )
    b_input, c_input = bc_input[:, 0], bc_input[:, 1]
    tail = jnp.concatenate(
        [x_input[rows - RIM :], b_input[rows - RIM :], c_input[rows - RIM :]], axis=1
    )
    rim = from_behind(tail, ("ctx", "tp"), 1)
    x_shift = x_bias.reshape(1, -1)
    conv_scratch = pltpu.VMEM((8 + rows, LANES), F32)
    traded = []
    for group in range(gd):
        parts = call(
            functools.partial(send_kernel, group, tp, gd),
            [
                x_input, b_input, dt_input, rim, x_kernel, x_shift, bc_kernel[:, 0],
                bc_bias[0:1],
            ],
            [shape(((X_TILES + 1) * rows + EXTRA, LANES), BF16)] * tp,
            [conv_scratch, pltpu.VMEM((HEADS, rows), F32)],
            name=f"send{group}",
        )
        traded.append(trade(parts))
    late = trade(
        call(
            functools.partial(last_send_kernel, tp, gd, kept),
            [z_input, c_input, rim, bc_kernel[:, 1], bc_bias[1:2]],
            [shape((rows, (gd - kept) * GROUP_WIDTH + gd * LANES), BF16)] * tp,
            [conv_scratch],
            name="send_last",
        )
    )
    held = []
    for group in range(gd):
        outs = [
            shape((ctx_rows, GROUP_WIDTH), BF16),
            shape((ctx_rows, GROUP_WIDTH), BF16),
            shape((ctx_rows, STATE_DIM), BF16),
            shape((tp, PER_GROUP, rows), F32),
            shape((spans, PER_GROUP, rows), F32),
            shape((spans, PER_GROUP, rows), F32),
            shape((STATE_DIM + EXTRA, GROUP_WIDTH), BF16),
        ]
        if spans > 1:
            outs.append(shape((spans, STATE_DIM, GROUP_WIDTH), F32))
        made = call(
            functools.partial(state_kernel, group, tp, spans),
            [dt_bias, a_log] + traded[group],
            outs,
            [pltpu.VMEM((tp, PER_GROUP, rows), F32)],
            scalars=2,
            name=f"state{group}",
        )
        kept_values = list(made[:6]) + list(made[7:])
        held.append((kept_values, scanned(made[6])))
    gain = norm_gain.reshape(1, -1)
    out = None
    for group in range(gd):
        values, sent = held[group]
        ins = [d_skip, gain] + (early if kept else [late[0]] * tp) + late + values + sent
        aliases = {}
        specs = smem(1) + [pl.BlockSpec((1, GROUP_WIDTH), lambda i, g=group: (0, g))]
        specs += vmem(len(ins) - 2)
        if group > 0:
            aliases = {len(ins): 0}
            ins.append(out)
            specs.append(pl.BlockSpec(memory_space=pl.ANY))
        out = pl.pallas_call(
            functools.partial(out_kernel, group, tp, gd, kept, spans, len(sent)),
            grid=(1,),
            in_specs=specs,
            out_specs=pl.BlockSpec((ctx_rows, GROUP_WIDTH), lambda i, g=group: (0, g)),
            out_shape=shape((ctx_rows, width), BF16),
            scratch_shapes=[pltpu.VMEM((spans, STATE_DIM, GROUP_WIDTH), BF16)],
            input_output_aliases=aliases,
            name=f"out{group}",
        )(*ins)
    return out


def solution(mesh):
    lead = ("groups", "ctx", "tp")
    in_specs = (
        P(lead, None), P(lead, None, None), P(lead, None), P(lead, None), P(), P(), P(), P(),
        P("tp"), P("tp"), P("tp"), P("tp"),
    )
    out_specs = P(("groups", "ctx"), "tp")
    return jax.shard_map(shards, mesh=mesh, in_specs=in_specs, out_specs=out_specs, check_vma=False)
```

```python
import functools

import jax
import jax.numpy as jnp
from jax import lax
from jax.experimental import pallas as pl
from jax.experimental.pallas import tpu as pltpu
from jax.sharding import PartitionSpec as P

HEADS = 64
HEAD_DIM = 64
STATE_DIM = 128
GROUPS = 8
CONV_TAPS = 4
PER_GROUP = HEADS // GROUPS
GROUP_WIDTH = PER_GROUP * HEAD_DIM
LANES = 128
X_TILES = GROUP_WIDTH // LANES
SPAN = 512
RIM = 4
EXTRA = 16
SHORT = pl.CostEstimate(flops=1, bytes_accessed=1, transcendentals=1)
LONG = pl.CostEstimate(flops=10**12, bytes_accessed=10**9, transcendentals=1)
ROOM = 12 * 2**20
F32 = jnp.float32
BF16 = jnp.bfloat16


def partner(place, slot):
    return place ^ slot


def swap(value, slot):
    return lax.ppermute(value, "tp", [(i, i ^ slot) for i in range(lax.axis_size("tp"))])


def from_behind(value, axis, steps):
    count = lax.axis_size(axis)
    return lax.ppermute(value, axis, [(i, i + steps) for i in range(count - steps)])


def in_three(value):
    high = value.astype(BF16).astype(F32)
    rest = value - high
    middle = rest.astype(BF16).astype(F32)
    low = rest - middle
    return jnp.concatenate([high, middle, low, jnp.zeros_like(value)], axis=0).astype(BF16)


def head_columns():
    rows = lax.broadcasted_iota(jnp.int32, (4 * PER_GROUP, GROUP_WIDTH), 0)
    columns = lax.broadcasted_iota(jnp.int32, (4 * PER_GROUP, GROUP_WIDTH), 1)
    own = lax.rem(rows, PER_GROUP) == lax.div(columns, HEAD_DIM)
    return jnp.where(own, 1.0, 0.0).astype(BF16)


def spread(value, columns):
    return lax.dot_general(
        in_three(value), columns, (((0,), (0,)), ((), ())), preferred_element_type=F32
    )


def column_of(ref, first, width=LANES):
    rows = lax.broadcasted_iota(jnp.int32, (PER_GROUP, width), 0)
    out = jnp.zeros((PER_GROUP, width), F32)
    for head in range(PER_GROUP):
        out = jnp.where(rows == head, ref[first + head], out)
    return out


def conv_tile(scratch, rim, rows, taps, shift):
    count = rows.shape[0]
    scratch[8 - RIM : 8, :] = rim.astype(F32)
    scratch[8 : 8 + count, :] = rows.astype(F32)
    total = shift + jnp.zeros((count, LANES), F32)
    for tap in range(CONV_TAPS):
        first = 8 - (CONV_TAPS - 1) + tap
        total = total + taps[tap : tap + 1, :] * scratch[first : first + count, :]
    return (total / (1.0 + jnp.exp(-total))).astype(BF16)


def rim_kernel(x_ref, bc_ref, out_ref):
    width = x_ref.shape[1]
    count = bc_ref.shape[2]
    rows = bc_ref.shape[0]
    out_ref[:, :width] = x_ref[x_ref.shape[0] - RIM :, :]
    for tile in range(count // LANES):
        at = slice(tile * LANES, (tile + 1) * LANES)
        both = bc_ref[:, :, at].astype(F32)
        for part in range(2):
            first = width + part * count + tile * LANES
            out_ref[:, first : first + LANES] = both[rows - RIM :, part, :].astype(BF16)


def load_kernel(count, *refs):
    sems = refs[-1]
    copies = [
        pltpu.make_async_copy(refs[place], refs[count + place], sems.at[place])
        for place in range(count)
    ]
    for copy in copies:
        copy.start()
    for copy in copies:
        copy.wait()


def conv_tile_of(scratch, rim_ref, bc_ref, taps_ref, shift_ref, part, first):
    at = pl.ds(pl.multiple_of(first, LANES), LANES)
    count = bc_ref.shape[2]
    rim_at = pl.ds(
        pl.multiple_of(rim_ref.shape[1] - (2 - part) * count + first, LANES), LANES
    )
    rows = bc_ref[:, :, at].astype(F32)[:, part, :]
    taps = taps_ref[:, :, at][:, part, :]
    return conv_tile(scratch, rim_ref[:, rim_at], rows, taps, shift_ref[part : part + 1, at])


def send_kernel(
    group, tp, gd, x_ref, bc_ref, dt_ref, rim_ref, tx_ref, sx_ref, tb_ref, sb_ref, *rest
):
    outs, scratch, dt_scr = rest[:tp], rest[tp], rest[tp + 1]
    rows = x_ref.shape[0]
    me = lax.axis_index("tp")
    dt_scr[...] = dt_ref[...].astype(F32)
    for slot in range(tp):
        out = outs[slot]
        whole = partner(me, slot) * gd + group
        for tile in range(X_TILES):
            at = pl.ds(pl.multiple_of(whole * GROUP_WIDTH + tile * LANES, LANES), LANES)
            out[tile * rows : (tile + 1) * rows, :] = conv_tile(
                scratch, rim_ref[:, at], x_ref[:, at], tx_ref[:, at], sx_ref[:, at]
            )
        out[X_TILES * rows : (X_TILES + 1) * rows, :] = conv_tile_of(
            scratch, rim_ref, bc_ref, tb_ref, sb_ref, 0, whole * STATE_DIM
        )
        mine = dt_scr[pl.ds(pl.multiple_of(whole * PER_GROUP, PER_GROUP), PER_GROUP), :]
        first = (X_TILES + 1) * rows
        out[first : first + EXTRA, :] = jnp.concatenate(
            [mine, jnp.zeros((EXTRA - PER_GROUP, rows), F32)], axis=0
        ).astype(BF16)
        if group == gd - 1:
            for other in range(gd):
                first = (X_TILES + 1 + other) * rows + EXTRA
                out[first : first + rows, :] = conv_tile_of(
                    scratch, rim_ref, bc_ref, tb_ref, sb_ref, 1,
                    (partner(me, slot) * gd + other) * STATE_DIM,
                )


def gate_kernel(z_ref, out_ref):
    tp, _, width = out_ref.shape
    for place in range(tp):
        out_ref[place] = z_ref[:, place * width : (place + 1) * width]


def state_kernel(group, tp, spans, bias_ref, log_ref, *rest):
    pieces = rest[:tp]
    conv_ref, scaled_ref, b_ref, grow_ref, mid_ref, prior_ref, ship_ref = rest[tp : tp + 7]
    ahead_ref = rest[tp + 7] if spans > 1 else None
    step_scr = rest[-1]
    rows = conv_ref.shape[0] // tp
    per_span = tp // spans
    me = lax.axis_index("tp")
    for slot in range(tp):
        place = partner(me, slot)
        at = pl.ds(pl.multiple_of(place * rows, rows), rows)
        for tile in range(X_TILES):
            conv_ref[at, tile * LANES : (tile + 1) * LANES] = pieces[slot][
                tile * rows : (tile + 1) * rows, :
            ]
        b_ref[at, :] = pieces[slot][X_TILES * rows : (X_TILES + 1) * rows, :]
        first = (X_TILES + 1) * rows
        step_scr[place] = pieces[slot][first : first + EXTRA, :].astype(F32)[:PER_GROUP]
    bias = column_of(bias_ref, group * PER_GROUP, rows)
    rate = jnp.exp(column_of(log_ref, group * PER_GROUP, rows))
    steps, logs = [], []
    for place in range(tp):
        raw = step_scr[place] + bias
        step = jnp.maximum(raw, 0.0) + jnp.log1p(jnp.exp(-jnp.abs(raw)))
        steps.append(step)
        logs.append(-step * rate)
    tri_r = lax.broadcasted_iota(jnp.int32, (rows, rows), 0)
    tri_c = lax.broadcasted_iota(jnp.int32, (rows, rows), 1)
    tri = jnp.where(tri_r <= tri_c, 1.0, 0.0).astype(BF16)
    parts = jnp.dot(in_three(jnp.concatenate(logs, axis=0)), tri, preferred_element_type=F32)
    count = tp * PER_GROUP
    sums = parts[:count] + parts[count : 2 * count] + parts[2 * count : 3 * count]
    columns = head_columns()
    prior = jnp.zeros((PER_GROUP, rows), F32)
    total = None
    for span in range(spans):
        inside, running = [], jnp.zeros((PER_GROUP, rows), F32)
        for piece in range(per_span):
            first = (span * per_span + piece) * PER_GROUP
            local = sums[first : first + PER_GROUP]
            inside.append(running + local)
            running = running + jnp.broadcast_to(local[:, rows - 1 :], (PER_GROUP, rows))
            if piece == max(per_span // 2 - 1, 0):
                middle = running
        for piece in range(per_span):
            place = span * per_span + piece
            grow_ref[place] = jnp.exp(inside[piece] - middle)
            scale = spread(jnp.exp(middle - inside[piece]) * steps[place], columns)
            at = slice(place * rows, (place + 1) * rows)
            scaled_ref[at, :] = (conv_ref[at, :].astype(F32) * scale).astype(BF16)
        at = slice(span * per_span * rows, (span + 1) * per_span * rows)
        summed = lax.dot_general(
            b_ref[at, :], scaled_ref[at, :], (((0,), (0,)), ((), ())), preferred_element_type=F32
        )
        summed = summed * spread(jnp.exp(running - middle), columns)
        mid_ref[span] = middle
        prior_ref[span] = prior
        if spans > 1:
            ahead_ref[span] = total if total is not None else jnp.zeros_like(summed)
        total = summed if total is None else total * spread(jnp.exp(running), columns) + summed
        prior = prior + running
    ship_ref[:STATE_DIM, :] = total.astype(BF16)
    decay = spread(jnp.exp(prior), columns)[:EXTRA]
    high = decay.astype(BF16).astype(F32)
    middle = (decay - high).astype(BF16).astype(F32)
    at = lax.broadcasted_iota(jnp.int32, (EXTRA, GROUP_WIDTH), 0)
    stacked = jnp.where(at == 0, high, jnp.where(at == 1, middle, decay - high - middle))
    ship_ref[STATE_DIM:, :] = jnp.where(at < 3, stacked, 0.0).astype(BF16)


def shipped(ref):
    rows = ref[STATE_DIM:, :].astype(F32)
    return ref[:STATE_DIM, :].astype(F32), rows[0:1] + rows[1:2] + rows[2:3]


def mix_kernel(gd, spans, tp, skip_ref, *rest):
    pieces, rest = rest[:tp], rest[tp:]
    held, outs = rest[: 4 * gd], rest[4 * gd :]
    rows = outs[0].shape[0] // tp
    per_span = tp // spans
    join = 2 if per_span % 2 == 0 else 1
    me = lax.axis_index("tp")
    columns = head_columns()
    for group in range(gd):
        conv_ref, scaled_ref, b_ref, grow_ref = held[4 * group : 4 * group + 4]
        c_ref, mixed_ref = outs[2 * group : 2 * group + 2]
        first = (X_TILES + 1 + group) * rows + EXTRA
        for slot in range(tp):
            at = pl.ds(pl.multiple_of(partner(me, slot) * rows, rows), rows)
            c_ref[at, :] = pieces[slot][first : first + rows, :]
        skip = spread(column_of(skip_ref, group * PER_GROUP), columns)[:1]
        for place in range(0, tp, join):
            span = place // per_span
            at = slice(place * rows, (place + join) * rows)
            inside = slice(span * per_span * rows, (place + join) * rows)
            scores = lax.dot_general(
                c_ref[at, :], b_ref[inside, :], (((1,), (1,)), ((), ())),
                preferred_element_type=F32,
            )
            t_at = lax.broadcasted_iota(jnp.int32, scores.shape, 0)
            s_at = lax.broadcasted_iota(jnp.int32, scores.shape, 1) - (at.start - inside.start)
            masked = jnp.where(s_at <= t_at, scores, 0.0).astype(BF16)
            mixed = jnp.dot(masked, scaled_ref[inside, :], preferred_element_type=F32)
            grow = [spread(grow_ref[other], columns) for other in range(place, place + join)]
            mixed = mixed * jnp.concatenate(grow, axis=0)
            mixed_ref[at, :] = mixed + skip * conv_ref[at, :].astype(F32)


def out_kernel(group, spans, states, gain_ref, gate_ref, c_ref, mixed_ref, grow_ref, *rest):
    mid_ref, prior_ref = rest[:2]
    rest = rest[2:]
    ahead_ref = None
    if spans > 1:
        ahead_ref, rest = rest[0], rest[1:]
    sent, rest = rest[:states], rest[states:]
    out_ref = rest[-1]
    tp, rows, _ = gate_ref.shape
    per_span = tp // spans
    columns = head_columns()
    state = None
    for ref in reversed(sent):
        value, decay = shipped(ref)
        state = value if state is None else state * decay + value
    join = 2 if per_span % 2 == 0 else 1
    for span in range(spans):
        start = state
        if spans > 1:
            start = start * spread(jnp.exp(prior_ref[span]), columns) + ahead_ref[span]
        start = (start * spread(jnp.exp(mid_ref[span]), columns)).astype(BF16)
        for first in range(span * per_span, (span + 1) * per_span, join):
            tall = join * rows
            at = slice(first * rows, first * rows + tall)
            carried = jnp.dot(c_ref[at, :], start, preferred_element_type=F32)
            grow = [spread(grow_ref[place], columns) for place in range(first, first + join)]
            mixed = mixed_ref[at, :] + carried * jnp.concatenate(grow, axis=0)
            z_at = group * GROUP_WIDTH
            gate = gate_ref[first : first + join, :, z_at : z_at + GROUP_WIDTH]
            gate = gate.reshape(tall, GROUP_WIDTH).astype(F32)
            gated = mixed * (gate / (1.0 + jnp.exp(-gate)))
            square = jnp.mean(gated * gated, axis=-1, keepdims=True)
            out_ref[at, :] = (gated * lax.rsqrt(square + 1e-5) * gain_ref[...]).astype(BF16)


def close(value):
    return pltpu.with_memory_space_constraint(value, pltpu.VMEM)


def far(value):
    return pltpu.with_memory_space_constraint(value, pltpu.HBM)


def vmem(count):
    return [pl.BlockSpec(memory_space=pltpu.VMEM)] * count


def smem(count):
    return [pl.BlockSpec(memory_space=pltpu.SMEM)] * count


def call(kernel, ins, outs, scratch, scalars=0, near=(), cost=LONG, name=None):
    ins = [close(value) if place in near else value for place, value in enumerate(ins)]
    outs = [pltpu.VMEM(out.shape, out.dtype) for out in outs]
    return pl.pallas_call(
        kernel,
        in_specs=smem(scalars) + vmem(len(ins) - scalars),
        out_specs=vmem(len(outs)),
        out_shape=outs,
        scratch_shapes=scratch,
        compiler_params=pltpu.CompilerParams(vmem_limit_bytes=ROOM),
        cost_estimate=cost,
        name=name,
    )(*ins)


def scanned(ship):
    count = lax.axis_size("ctx")
    if count <= 4:
        return [from_behind(ship, "ctx", steps) for steps in range(1, count)]
    state = ship[:STATE_DIM].astype(F32)
    decay = jnp.sum(ship[STATE_DIM : STATE_DIM + 3].astype(F32), axis=0, keepdims=True)

    def packed(state, decay):
        high = decay.astype(BF16).astype(F32)
        middle = (decay - high).astype(BF16).astype(F32)
        rows = [state, high, middle, decay - high - middle]
        rows.append(jnp.zeros((EXTRA - 3, GROUP_WIDTH), F32))
        return jnp.concatenate(rows, axis=0).astype(BF16)

    steps = 1
    while steps < count:
        other = from_behind(packed(state, decay), "ctx", steps)
        state = other[:STATE_DIM].astype(F32) * decay + state
        decay = decay * jnp.sum(
            other[STATE_DIM : STATE_DIM + 3].astype(F32), axis=0, keepdims=True
        )
        steps *= 2
    return [from_behind(packed(state, decay), "ctx", 1)]


def shards(
    x_input, bc_input, z_input, dt_input, x_kernel, x_bias, bc_kernel, bc_bias, dt_bias, a_log,
    d_skip, norm_gain,
):
    tp = lax.axis_size("tp")
    rows = x_input.shape[0]
    ctx_rows = rows * tp
    gd = GROUPS // tp
    spans = max(1, ctx_rows // SPAN)
    width = gd * GROUP_WIDTH
    shape = jax.ShapeDtypeStruct

    def trade(parts):
        return [parts[0]] + [swap(parts[slot], slot) for slot in range(1, tp)]

    count = bc_input.shape[2]
    every = x_input.shape[1] + 2 * count
    tail = pl.pallas_call(
        rim_kernel,
        grid=(1,),
        in_specs=[
            pl.BlockSpec((16, x_input.shape[1]), lambda i: (rows // 16 - 1, 0)),
            pl.BlockSpec((8, 2, count), lambda i: (rows // 8 - 1, 0, 0)),
        ],
        out_specs=pl.BlockSpec((RIM, every), lambda i: (0, 0)),
        out_shape=shape((RIM, every), BF16),
        compiler_params=pltpu.CompilerParams(vmem_limit_bytes=ROOM),
        name="rim",
    )(far(x_input), far(bc_input))
    rim = from_behind(tail, ("ctx", "tp"), 1)
    used = [
        far(value)
        for value in (
            x_input, bc_input, dt_input.T, x_kernel, x_bias.reshape(1, -1), bc_kernel, bc_bias
        )
    ]
    x_near, bc_near, *others = pl.pallas_call(
        functools.partial(load_kernel, len(used)),
        in_specs=[pl.BlockSpec(memory_space=pltpu.HBM)] * len(used),
        out_specs=vmem(len(used)),
        out_shape=[pltpu.VMEM(value.shape, value.dtype) for value in used],
        scratch_shapes=[pltpu.SemaphoreType.DMA((len(used),))],
        compiler_params=pltpu.CompilerParams(vmem_limit_bytes=ROOM),
        cost_estimate=LONG,
        name="load",
    )(*used)
    conv_scratch = pltpu.VMEM((8 + rows, LANES), F32)
    gates = call(
        gate_kernel, [z_input], [shape((tp, rows, width), BF16)], [], cost=SHORT, name="gates"
    )[0]
    traded = []
    for group in range(gd):
        tall = (X_TILES + 1 + (gd if group == gd - 1 else 0)) * rows + EXTRA
        parts = call(
            functools.partial(send_kernel, group, tp, gd),
            [x_near, bc_near, others[0], rim] + others[1:],
            [shape((tall, LANES), BF16)] * tp,
            [conv_scratch, pltpu.VMEM((HEADS, rows), F32)],
            near=range(8),
            name=f"send{group}",
        )
        rim, parts = lax.optimization_barrier((rim, parts))
        traded.append(trade(parts))
    gates, traded[-1][1] = lax.optimization_barrier((gates, traded[-1][1]))
    held = []
    for group in range(gd):
        outs = [
            shape((ctx_rows, GROUP_WIDTH), BF16),
            shape((ctx_rows, GROUP_WIDTH), BF16),
            shape((ctx_rows, STATE_DIM), BF16),
            shape((tp, PER_GROUP, rows), F32),
            shape((spans, PER_GROUP, rows), F32),
            shape((spans, PER_GROUP, rows), F32),
            shape((STATE_DIM + EXTRA, GROUP_WIDTH), BF16),
        ]
        if spans > 1:
            outs.append(shape((spans, STATE_DIM, GROUP_WIDTH), F32))
        made = call(
            functools.partial(state_kernel, group, tp, spans),
            [dt_bias, a_log] + traded[group],
            outs,
            [pltpu.VMEM((tp, PER_GROUP, rows), F32)],
            scalars=2,
            near=range(2, 2 + tp),
            cost=LONG if group == 0 else SHORT,
            name=f"state{group}",
        )
        ship = made[6]
        kept_values = list(made[:6]) + list(made[7:])
        held.append((kept_values, scanned(ship)))
    gates = lax.all_to_all(gates, "tp", split_axis=0, concat_axis=0, tiled=True)
    gain = norm_gain.reshape(1, -1)
    ins = [d_skip] + traded[-1]
    for values, _ in held:
        ins += values[:4]
    mixed = call(
        functools.partial(mix_kernel, gd, spans, tp),
        ins,
        [shape((ctx_rows, STATE_DIM), BF16), shape((ctx_rows, GROUP_WIDTH), F32)] * gd,
        [],
        scalars=1,
        near=range(1, len(ins)),
        cost=SHORT,
        name="mix",
    )
    out = None
    for group in range(gd):
        values, sent = held[group]
        ins = [gates, mixed[2 * group], mixed[2 * group + 1]] + values[3:] + sent
        ins = [gain] + [close(value) for value in ins]
        aliases = {}
        specs = [pl.BlockSpec((1, GROUP_WIDTH), lambda i, g=group: (0, g))]
        specs += vmem(len(ins) - 1)
        if group > 0:
            aliases = {len(ins): 0}
            ins.append(out)
            specs.append(pl.BlockSpec(memory_space=pl.ANY))
        out = pl.pallas_call(
            functools.partial(out_kernel, group, spans, len(sent)),
            grid=(1,),
            in_specs=specs,
            out_specs=pl.BlockSpec((ctx_rows, GROUP_WIDTH), lambda i, g=group: (0, g)),
            out_shape=shape((ctx_rows, width), BF16),
            input_output_aliases=aliases,
            compiler_params=pltpu.CompilerParams(vmem_limit_bytes=ROOM),
            cost_estimate=LONG,
            name=f"out{group}",
        )(*ins)
    return out


def solution(mesh):
    lead = ("groups", "ctx", "tp")
    in_specs = (
        P(lead, None), P(lead, None, None), P(lead, None), P(lead, None), P(), P(), P(), P(),
        P("tp"), P("tp"), P("tp"), P("tp"),
    )
    out_specs = P(("groups", "ctx"), "tp")
    return jax.shard_map(shards, mesh=mesh, in_specs=in_specs, out_specs=out_specs, check_vma=False)
```

```python
import functools

import jax
import jax.numpy as jnp
from jax import lax
from jax.experimental import pallas as pl
from jax.experimental.pallas import tpu as pltpu
from jax.sharding import PartitionSpec as P

HEADS = 64
HEAD_DIM = 64
STATE_DIM = 128
GROUPS = 8
CONV_TAPS = 4
PER_GROUP = HEADS // GROUPS
GROUP_WIDTH = PER_GROUP * HEAD_DIM
LANES = 128
X_TILES = GROUP_WIDTH // LANES
SPAN = 512
RIM = 4
EXTRA = 16
SHORT = pl.CostEstimate(flops=1, bytes_accessed=1, transcendentals=1)
LONG = pl.CostEstimate(flops=10**12, bytes_accessed=1, transcendentals=1)
ROOM = 12 * 2**20
COSTS = {"gates": SHORT, "state0": LONG, "state1": LONG, "mix": LONG}
F32 = jnp.float32
BF16 = jnp.bfloat16


def partner(place, slot):
    return place ^ slot


def swap(value, slot):
    return lax.ppermute(value, "tp", [(i, i ^ slot) for i in range(lax.axis_size("tp"))])


def from_behind(value, axis, steps):
    count = lax.axis_size(axis)
    return lax.ppermute(value, axis, [(i, i + steps) for i in range(count - steps)])


def in_three(value):
    high = value.astype(BF16).astype(F32)
    rest = value - high
    middle = rest.astype(BF16).astype(F32)
    low = rest - middle
    return jnp.concatenate([high, middle, low, jnp.zeros_like(value)], axis=0).astype(BF16)


def head_columns():
    rows = lax.broadcasted_iota(jnp.int32, (4 * PER_GROUP, GROUP_WIDTH), 0)
    columns = lax.broadcasted_iota(jnp.int32, (4 * PER_GROUP, GROUP_WIDTH), 1)
    own = lax.rem(rows, PER_GROUP) == lax.div(columns, HEAD_DIM)
    return jnp.where(own, 1.0, 0.0).astype(BF16)


def spread(value, columns):
    return lax.dot_general(
        in_three(value), columns, (((0,), (0,)), ((), ())), preferred_element_type=F32
    )


def spread_rows(value, columns):
    return lax.dot_general(
        columns, in_three(value), (((0,), (0,)), ((), ())), preferred_element_type=F32
    )


def column_of(ref, first, width=LANES):
    rows = lax.broadcasted_iota(jnp.int32, (PER_GROUP, width), 0)
    out = jnp.zeros((PER_GROUP, width), F32)
    for head in range(PER_GROUP):
        out = jnp.where(rows == head, ref[first + head], out)
    return out


def conv_tile(scratch, rim, rows, taps, shift):
    count = rows.shape[0]
    scratch[8 - RIM : 8, :] = rim.astype(F32)
    scratch[8 : 8 + count, :] = rows.astype(F32)
    total = shift + jnp.zeros((count, LANES), F32)
    for tap in range(CONV_TAPS):
        first = 8 - (CONV_TAPS - 1) + tap
        total = total + taps[tap : tap + 1, :] * scratch[first : first + count, :]
    return (total / (1.0 + jnp.exp(-total))).astype(BF16)


def rim_kernel(x_ref, bc_ref, out_ref):
    width = x_ref.shape[1]
    count = bc_ref.shape[2]
    rows = bc_ref.shape[0]
    out_ref[:, :width] = x_ref[x_ref.shape[0] - RIM :, :]
    for tile in range(count // LANES):
        at = slice(tile * LANES, (tile + 1) * LANES)
        both = bc_ref[:, :, at].astype(F32)
        for part in range(2):
            first = width + part * count + tile * LANES
            out_ref[:, first : first + LANES] = both[rows - RIM :, part, :].astype(BF16)


def load_kernel(count, *refs):
    sems = refs[-1]
    copies = [
        pltpu.make_async_copy(refs[place], refs[count + place], sems.at[place])
        for place in range(count)
    ]
    for copy in copies:
        copy.start()
    for copy in copies:
        copy.wait()


def conv_tile_of(scratch, rim_ref, bc_ref, taps_ref, shift_ref, part, first):
    at = pl.ds(pl.multiple_of(first, LANES), LANES)
    count = bc_ref.shape[2]
    rim_at = pl.ds(
        pl.multiple_of(rim_ref.shape[1] - (2 - part) * count + first, LANES), LANES
    )
    rows = bc_ref[:, :, at].astype(F32)[:, part, :]
    taps = taps_ref[:, :, at][:, part, :]
    return conv_tile(scratch, rim_ref[:, rim_at], rows, taps, shift_ref[part : part + 1, at])


def send_kernel(
    group, tp, gd, x_ref, bc_ref, dt_ref, rim_ref, tx_ref, sx_ref, tb_ref, sb_ref, *rest
):
    outs, scratch, dt_scr = rest[:tp], rest[tp], rest[tp + 1]
    rows = x_ref.shape[0]
    me = lax.axis_index("tp")
    dt_scr[...] = dt_ref[...].astype(F32)
    for slot in range(tp):
        out = outs[slot]
        whole = partner(me, slot) * gd + group
        for tile in range(X_TILES):
            at = pl.ds(pl.multiple_of(whole * GROUP_WIDTH + tile * LANES, LANES), LANES)
            out[tile * rows : (tile + 1) * rows, :] = conv_tile(
                scratch, rim_ref[:, at], x_ref[:, at], tx_ref[:, at], sx_ref[:, at]
            )
        out[X_TILES * rows : (X_TILES + 1) * rows, :] = conv_tile_of(
            scratch, rim_ref, bc_ref, tb_ref, sb_ref, 0, whole * STATE_DIM
        )
        mine = dt_scr[pl.ds(pl.multiple_of(whole * PER_GROUP, PER_GROUP), PER_GROUP), :]
        first = (X_TILES + 1) * rows
        out[first : first + EXTRA, :] = jnp.concatenate(
            [mine, jnp.zeros((EXTRA - PER_GROUP, rows), F32)], axis=0
        ).astype(BF16)
        if group == gd - 1:
            for other in range(gd):
                first = (X_TILES + 1 + other) * rows + EXTRA
                out[first : first + rows, :] = conv_tile_of(
                    scratch, rim_ref, bc_ref, tb_ref, sb_ref, 1,
                    (partner(me, slot) * gd + other) * STATE_DIM,
                )


def gate_kernel(z_ref, out_ref):
    tp, _, width = out_ref.shape
    for place in range(tp):
        out_ref[place] = z_ref[:, place * width : (place + 1) * width]


def state_kernel(group, tp, spans, bias_ref, log_ref, *rest):
    pieces = rest[:tp]
    conv_ref, scaled_ref, b_ref, grow_ref, mid_ref, prior_ref, ship_ref = rest[tp : tp + 7]
    ahead_ref = rest[tp + 7] if spans > 1 else None
    step_scr = rest[-1]
    rows = conv_ref.shape[0] // tp
    per_span = tp // spans
    me = lax.axis_index("tp")
    for slot in range(tp):
        place = partner(me, slot)
        at = pl.ds(pl.multiple_of(place * rows, rows), rows)
        for tile in range(X_TILES):
            conv_ref[at, tile * LANES : (tile + 1) * LANES] = pieces[slot][
                tile * rows : (tile + 1) * rows, :
            ]
        b_ref[at, :] = pieces[slot][X_TILES * rows : (X_TILES + 1) * rows, :]
        first = (X_TILES + 1) * rows
        step_scr[place] = pieces[slot][first : first + EXTRA, :].astype(F32)[:PER_GROUP]
    bias = column_of(bias_ref, group * PER_GROUP, rows)
    rate = jnp.exp(column_of(log_ref, group * PER_GROUP, rows))
    steps, logs = [], []
    for place in range(tp):
        raw = step_scr[place] + bias
        step = jnp.maximum(raw, 0.0) + jnp.log1p(jnp.exp(-jnp.abs(raw)))
        steps.append(step)
        logs.append(-step * rate)
    tri_r = lax.broadcasted_iota(jnp.int32, (rows, rows), 0)
    tri_c = lax.broadcasted_iota(jnp.int32, (rows, rows), 1)
    tri = jnp.where(tri_r <= tri_c, 1.0, 0.0).astype(BF16)
    parts = jnp.dot(in_three(jnp.concatenate(logs, axis=0)), tri, preferred_element_type=F32)
    count = tp * PER_GROUP
    sums = parts[:count] + parts[count : 2 * count] + parts[2 * count : 3 * count]
    columns = head_columns()
    prior = jnp.zeros((PER_GROUP, rows), F32)
    total = None
    for span in range(spans):
        inside, running = [], jnp.zeros((PER_GROUP, rows), F32)
        for piece in range(per_span):
            first = (span * per_span + piece) * PER_GROUP
            local = sums[first : first + PER_GROUP]
            inside.append(running + local)
            running = running + jnp.broadcast_to(local[:, rows - 1 :], (PER_GROUP, rows))
            if piece == max(per_span // 2 - 1, 0):
                middle = running
        for piece in range(per_span):
            place = span * per_span + piece
            grow_ref[place] = jnp.exp(inside[piece] - middle)
            scale = spread(jnp.exp(middle - inside[piece]) * steps[place], columns)
            at = slice(place * rows, (place + 1) * rows)
            scaled_ref[at, :] = (conv_ref[at, :].astype(F32) * scale).astype(BF16)
        at = slice(span * per_span * rows, (span + 1) * per_span * rows)
        summed = lax.dot_general(
            scaled_ref[at, :], b_ref[at, :], (((0,), (0,)), ((), ())), preferred_element_type=F32
        )
        summed = summed * spread_rows(jnp.exp(running - middle), columns)
        mid_ref[span] = middle
        prior_ref[span] = prior
        if spans > 1:
            ahead_ref[span] = total if total is not None else jnp.zeros_like(summed)
        total = summed if total is None else total * spread_rows(jnp.exp(running), columns) + summed
        prior = prior + running
    ship_ref[:GROUP_WIDTH, :] = total.astype(BF16)
    decay = jnp.exp(prior)
    high = decay.astype(BF16).astype(F32)
    ship_ref[GROUP_WIDTH:, :] = jnp.concatenate([high, decay - high], axis=0).astype(BF16)


def shipped(ref):
    rows = ref[GROUP_WIDTH:, :].astype(F32)
    return ref[:GROUP_WIDTH, :].astype(F32), rows[:PER_GROUP] + rows[PER_GROUP:]


def mix_kernel(gd, spans, tp, skip_ref, gate_ref, *rest):
    pieces, rest = rest[:tp], rest[tp:]
    held, outs = rest[: 4 * gd], rest[4 * gd :]
    rows = outs[0].shape[0] // tp
    per_span = tp // spans
    join = 2 if per_span % 2 == 0 else 1
    me = lax.axis_index("tp")
    columns = head_columns()
    for group in range(gd):
        conv_ref, scaled_ref, b_ref, grow_ref = held[4 * group : 4 * group + 4]
        c_ref, plain_ref, slope_ref = outs[3 * group : 3 * group + 3]
        first = (X_TILES + 1 + group) * rows + EXTRA
        for slot in range(tp):
            at = pl.ds(pl.multiple_of(partner(me, slot) * rows, rows), rows)
            c_ref[at, :] = pieces[slot][first : first + rows, :]
        skip = spread(column_of(skip_ref, group * PER_GROUP), columns)[:1]
        for place in range(0, tp, join):
            span = place // per_span
            at = slice(place * rows, (place + join) * rows)
            inside = slice(span * per_span * rows, (place + join) * rows)
            scores = lax.dot_general(
                c_ref[at, :], b_ref[inside, :], (((1,), (1,)), ((), ())),
                preferred_element_type=F32,
            )
            t_at = lax.broadcasted_iota(jnp.int32, scores.shape, 0)
            s_at = lax.broadcasted_iota(jnp.int32, scores.shape, 1) - (at.start - inside.start)
            masked = jnp.where(s_at <= t_at, scores, 0.0).astype(BF16)
            mixed = jnp.dot(masked, scaled_ref[inside, :], preferred_element_type=F32)
            grow = jnp.concatenate(
                [spread(grow_ref[other], columns) for other in range(place, place + join)], axis=0
            )
            mixed = mixed * grow + skip * conv_ref[at, :].astype(F32)
            z_at = group * GROUP_WIDTH
            gate = gate_ref[place : place + join, :, z_at : z_at + GROUP_WIDTH]
            gate = gate.reshape(join * rows, GROUP_WIDTH).astype(F32)
            gate = gate / (1.0 + jnp.exp(-gate))
            plain_ref[at, :] = mixed * gate
            slope_ref[at, :] = grow * gate


def out_kernel(spans, states, gain_ref, c_ref, plain_ref, slope_ref, *rest):
    mid_ref, prior_ref = rest[:2]
    rest = rest[2:]
    ahead_ref = None
    if spans > 1:
        ahead_ref, rest = rest[0], rest[1:]
    sent, rest = rest[:states], rest[states:]
    out_ref = rest[-1]
    columns = head_columns()
    ctx = lax.axis_index("ctx")
    state = None
    for steps in range(states, 0, -1):
        value, decay = shipped(sent[steps - 1])
        value = jnp.where(ctx >= steps, value, 0.0)
        state = value if state is None else state * spread_rows(decay, columns) + value
    span_rows = c_ref.shape[0] // spans
    tall = min(span_rows, 256)
    for span in range(spans):
        start = state
        if spans > 1:
            start = start * spread_rows(jnp.exp(prior_ref[span]), columns) + ahead_ref[span]
        start = (start * spread_rows(jnp.exp(mid_ref[span]), columns)).astype(BF16)
        for first in range(span * span_rows, (span + 1) * span_rows, tall):
            at = slice(first, first + tall)
            carried = lax.dot_general(
                c_ref[at, :], start, (((1,), (1,)), ((), ())), preferred_element_type=F32
            )
            gated = plain_ref[at, :] + carried * slope_ref[at, :]
            square = jnp.mean(gated * gated, axis=-1, keepdims=True)
            out_ref[at, :] = (gated * lax.rsqrt(square + 1e-5) * gain_ref[...]).astype(BF16)


def close(value):
    return pltpu.with_memory_space_constraint(value, pltpu.VMEM)


def far(value):
    return pltpu.with_memory_space_constraint(value, pltpu.HBM)


def vmem(count):
    return [pl.BlockSpec(memory_space=pltpu.VMEM)] * count


def smem(count):
    return [pl.BlockSpec(memory_space=pltpu.SMEM)] * count


def call(kernel, ins, outs, scratch, scalars=0, near=(), name=None):
    ins = [close(value) if place in near else value for place, value in enumerate(ins)]
    outs = [pltpu.VMEM(out.shape, out.dtype) for out in outs]
    return pl.pallas_call(
        kernel,
        in_specs=smem(scalars) + vmem(len(ins) - scalars),
        out_specs=vmem(len(outs)),
        out_shape=outs,
        scratch_shapes=scratch,
        compiler_params=pltpu.CompilerParams(vmem_limit_bytes=ROOM),
        cost_estimate=COSTS.get(name, LONG),
        name=name,
    )(*ins)


def joined(ship):
    rows = ship[GROUP_WIDTH:].astype(F32)
    return rows[:PER_GROUP] + rows[PER_GROUP:]


def packed(state, decay):
    high = decay.astype(BF16).astype(F32)
    return jnp.concatenate([state, high, decay - high], axis=0).astype(BF16)


def scanned(ship):
    count = lax.axis_size("ctx")
    if count <= 4:
        return [
            lax.ppermute(ship, "ctx", [(i, (i + steps) % count) for i in range(count)])
            for steps in range(1, count)
        ]
    state, decay = ship[:GROUP_WIDTH].astype(F32), joined(ship)
    steps = 1
    while steps < count:
        other = from_behind(packed(state, decay), "ctx", steps)
        scale = jnp.repeat(decay, HEAD_DIM, axis=0)
        state = other[:GROUP_WIDTH].astype(F32) * scale + state
        decay = decay * joined(other)
        steps *= 2
    return [from_behind(packed(state, decay), "ctx", 1)]


def shards(
    x_input, bc_input, z_input, dt_input, x_kernel, x_bias, bc_kernel, bc_bias, dt_bias, a_log,
    d_skip, norm_gain,
):
    tp = lax.axis_size("tp")
    rows = x_input.shape[0]
    ctx_rows = rows * tp
    gd = GROUPS // tp
    spans = max(1, ctx_rows // SPAN)
    width = gd * GROUP_WIDTH
    shape = jax.ShapeDtypeStruct

    def trade(parts):
        return [parts[0]] + [swap(parts[slot], slot) for slot in range(1, tp)]

    count = bc_input.shape[2]
    every = x_input.shape[1] + 2 * count
    tail = pl.pallas_call(
        rim_kernel,
        grid=(1,),
        in_specs=[
            pl.BlockSpec((16, x_input.shape[1]), lambda i: (rows // 16 - 1, 0)),
            pl.BlockSpec((8, 2, count), lambda i: (rows // 8 - 1, 0, 0)),
        ],
        out_specs=pl.BlockSpec((RIM, every), lambda i: (0, 0)),
        out_shape=shape((RIM, every), BF16),
        compiler_params=pltpu.CompilerParams(vmem_limit_bytes=ROOM),
        name="rim",
    )(far(x_input), far(bc_input))
    rim = from_behind(tail, ("ctx", "tp"), 1)
    used = [
        far(value)
        for value in (
            x_input, bc_input, dt_input.T, x_kernel, x_bias.reshape(1, -1), bc_kernel, bc_bias
        )
    ]
    x_near, bc_near, *others = pl.pallas_call(
        functools.partial(load_kernel, len(used)),
        in_specs=[pl.BlockSpec(memory_space=pltpu.HBM)] * len(used),
        out_specs=vmem(len(used)),
        out_shape=[pltpu.VMEM(value.shape, value.dtype) for value in used],
        scratch_shapes=[pltpu.SemaphoreType.DMA((len(used),))],
        compiler_params=pltpu.CompilerParams(vmem_limit_bytes=ROOM),
        cost_estimate=LONG,
        name="load",
    )(*used)
    conv_scratch = pltpu.VMEM((8 + rows, LANES), F32)
    traded = []
    for group in range(gd):
        tall = (X_TILES + 1 + (gd if group == gd - 1 else 0)) * rows + EXTRA
        parts = call(
            functools.partial(send_kernel, group, tp, gd),
            [x_near, bc_near, others[0], rim] + others[1:],
            [shape((tall, LANES), BF16)] * tp,
            [conv_scratch, pltpu.VMEM((HEADS, rows), F32)],
            near=range(8),
            name=f"send{group}",
        )
        rim, parts, z_input = lax.optimization_barrier((rim, parts, z_input))
        traded.append(trade(parts))
        if group == 0:
            gates = call(
                gate_kernel, [z_input], [shape((tp, rows, width), BF16)], [], name="gates"
            )[0]
    gates, traded[0][tp // 2] = lax.optimization_barrier((gates, traded[0][tp // 2]))
    held = []
    for group in range(gd):
        outs = [
            shape((ctx_rows, GROUP_WIDTH), BF16),
            shape((ctx_rows, GROUP_WIDTH), BF16),
            shape((ctx_rows, STATE_DIM), BF16),
            shape((tp, PER_GROUP, rows), F32),
            shape((spans, PER_GROUP, rows), F32),
            shape((spans, PER_GROUP, rows), F32),
            shape((GROUP_WIDTH + 2 * PER_GROUP, STATE_DIM), BF16),
        ]
        if spans > 1:
            outs.append(shape((spans, GROUP_WIDTH, STATE_DIM), F32))
        made = call(
            functools.partial(state_kernel, group, tp, spans),
            [far(dt_bias), far(a_log)] + traded[group],
            outs,
            [pltpu.VMEM((tp, PER_GROUP, rows), F32)],
            scalars=2,
            near=range(2, 2 + tp),
            name=f"state{group}",
        )
        ship = made[6]
        kept_values = list(made[:6]) + list(made[7:])
        held.append((kept_values, scanned(ship)))
    gates = lax.all_to_all(gates, "tp", split_axis=0, concat_axis=0, tiled=True)
    if gd > 1:
        first = held[0][1]
        gates, first[0] = lax.optimization_barrier((gates, first[0]))
    gain = far(norm_gain.reshape(1, -1))
    ins = [far(d_skip), gates] + traded[-1]
    for values, _ in held:
        ins += values[:4]
    mixed = call(
        functools.partial(mix_kernel, gd, spans, tp),
        ins,
        ([shape((ctx_rows, STATE_DIM), BF16)] + [shape((ctx_rows, GROUP_WIDTH), F32)] * 2) * gd,
        [],
        scalars=1,
        near=range(1, len(ins)),
        name="mix",
    )
    out = None
    for group in range(gd):
        values, sent = held[group]
        ins = list(mixed[3 * group : 3 * group + 3]) + values[4:] + sent
        ins = [gain] + [close(value) for value in ins]
        aliases = {}
        specs = [pl.BlockSpec((1, GROUP_WIDTH), lambda i, g=group: (0, g))]
        specs += vmem(len(ins) - 1)
        if group > 0:
            aliases = {len(ins): 0}
            ins.append(out)
            specs.append(pl.BlockSpec(memory_space=pl.ANY))
        out = pl.pallas_call(
            functools.partial(out_kernel, spans, len(sent)),
            grid=(1,),
            in_specs=specs,
            out_specs=pl.BlockSpec((ctx_rows, GROUP_WIDTH), lambda i, g=group: (0, g)),
            out_shape=shape((ctx_rows, width), BF16),
            input_output_aliases=aliases,
            compiler_params=pltpu.CompilerParams(vmem_limit_bytes=ROOM),
            cost_estimate=LONG,
            name=f"out{group}",
        )(*ins)
    return out


def solution(mesh):
    lead = ("groups", "ctx", "tp")
    in_specs = (
        P(lead, None), P(lead, None, None), P(lead, None), P(lead, None), P(), P(), P(), P(),
        P("tp"), P("tp"), P("tp"), P("tp"),
    )
    out_specs = P(("groups", "ctx"), "tp")
    return jax.shard_map(shards, mesh=mesh, in_specs=in_specs, out_specs=out_specs, check_vma=False)
```

```python
import functools

import jax
import jax.numpy as jnp
from jax import lax
from jax.experimental import pallas as pl
from jax.experimental.pallas import tpu as pltpu
from jax.sharding import PartitionSpec as P

HEADS = 64
HEAD_DIM = 64
STATE_DIM = 128
GROUPS = 8
CONV_TAPS = 4
PER_GROUP = HEADS // GROUPS
GROUP_WIDTH = PER_GROUP * HEAD_DIM
LANES = 128
X_TILES = GROUP_WIDTH // LANES
SPAN = 512
RIM = 4
EXTRA = 16
SHORT = pl.CostEstimate(flops=1, bytes_accessed=1, transcendentals=1)
LONG = pl.CostEstimate(flops=10**12, bytes_accessed=1, transcendentals=1)
ROOM = 12 * 2**20
COSTS = {"gates": SHORT, "state0": LONG, "state1": LONG, "mix": LONG}
F32 = jnp.float32
BF16 = jnp.bfloat16


def partner(place, slot):
    return place ^ slot


def swap(value, slot):
    return lax.ppermute(value, "tp", [(i, i ^ slot) for i in range(lax.axis_size("tp"))])


def from_behind(value, axis, steps):
    count = lax.axis_size(axis)
    return lax.ppermute(value, axis, [(i, i + steps) for i in range(count - steps)])


def in_three(value):
    high = value.astype(BF16).astype(F32)
    rest = value - high
    middle = rest.astype(BF16).astype(F32)
    low = rest - middle
    return jnp.concatenate([high, middle, low, jnp.zeros_like(value)], axis=0).astype(BF16)


def head_columns():
    rows = lax.broadcasted_iota(jnp.int32, (4 * PER_GROUP, GROUP_WIDTH), 0)
    columns = lax.broadcasted_iota(jnp.int32, (4 * PER_GROUP, GROUP_WIDTH), 1)
    own = lax.rem(rows, PER_GROUP) == lax.div(columns, HEAD_DIM)
    return jnp.where(own, 1.0, 0.0).astype(BF16)


def spread(value, columns):
    return lax.dot_general(
        in_three(value), columns, (((0,), (0,)), ((), ())), preferred_element_type=F32
    )


def spread_rows(value, columns):
    return lax.dot_general(
        columns, in_three(value), (((0,), (0,)), ((), ())), preferred_element_type=F32
    )


def column_of(ref, first, width=LANES):
    rows = lax.broadcasted_iota(jnp.int32, (PER_GROUP, width), 0)
    out = jnp.zeros((PER_GROUP, width), F32)
    for head in range(PER_GROUP):
        out = jnp.where(rows == head, ref[first + head], out)
    return out


def conv_tile(scratch, rim, rows, taps, shift):
    count = rows.shape[0]
    scratch[8 - RIM : 8, :] = rim.astype(F32)
    scratch[8 : 8 + count, :] = rows.astype(F32)
    total = shift + jnp.zeros((count, LANES), F32)
    for tap in range(CONV_TAPS):
        first = 8 - (CONV_TAPS - 1) + tap
        total = total + taps[tap : tap + 1, :] * scratch[first : first + count, :]
    return (total / (1.0 + jnp.exp(-total))).astype(BF16)


def rim_kernel(x_ref, bc_ref, out_ref):
    width = x_ref.shape[1]
    count = bc_ref.shape[2]
    rows = bc_ref.shape[0]
    out_ref[:, :width] = x_ref[x_ref.shape[0] - RIM :, :]
    for tile in range(count // LANES):
        at = slice(tile * LANES, (tile + 1) * LANES)
        both = bc_ref[:, :, at].astype(F32)
        for part in range(2):
            first = width + part * count + tile * LANES
            out_ref[:, first : first + LANES] = both[rows - RIM :, part, :].astype(BF16)


def load_kernel(count, *refs):
    sems = refs[-1]
    copies = [
        pltpu.make_async_copy(refs[place], refs[count + place], sems.at[place])
        for place in range(count)
    ]
    for copy in copies:
        copy.start()
    for copy in copies:
        copy.wait()


def conv_tile_of(scratch, rim_ref, bc_ref, taps_ref, shift_ref, part, first):
    at = pl.ds(pl.multiple_of(first, LANES), LANES)
    count = bc_ref.shape[2]
    rim_at = pl.ds(
        pl.multiple_of(rim_ref.shape[1] - (2 - part) * count + first, LANES), LANES
    )
    rows = bc_ref[:, :, at].astype(F32)[:, part, :]
    taps = taps_ref[:, :, at][:, part, :]
    return conv_tile(scratch, rim_ref[:, rim_at], rows, taps, shift_ref[part : part + 1, at])


def send_kernel(
    group, tp, gd, x_ref, bc_ref, dt_ref, rim_ref, tx_ref, sx_ref, tb_ref, sb_ref, *rest
):
    outs, scratch, dt_scr = rest[:tp], rest[tp], rest[tp + 1]
    rows = x_ref.shape[0]
    me = lax.axis_index("tp")
    dt_scr[...] = dt_ref[...].astype(F32)
    for slot in range(tp):
        out = outs[slot]
        whole = partner(me, slot) * gd + group
        for tile in range(X_TILES):
            at = pl.ds(pl.multiple_of(whole * GROUP_WIDTH + tile * LANES, LANES), LANES)
            out[tile * rows : (tile + 1) * rows, :] = conv_tile(
                scratch, rim_ref[:, at], x_ref[:, at], tx_ref[:, at], sx_ref[:, at]
            )
        out[X_TILES * rows : (X_TILES + 1) * rows, :] = conv_tile_of(
            scratch, rim_ref, bc_ref, tb_ref, sb_ref, 0, whole * STATE_DIM
        )
        mine = dt_scr[pl.ds(pl.multiple_of(whole * PER_GROUP, PER_GROUP), PER_GROUP), :]
        first = (X_TILES + 1) * rows
        out[first : first + EXTRA, :] = jnp.concatenate(
            [mine, jnp.zeros((EXTRA - PER_GROUP, rows), F32)], axis=0
        ).astype(BF16)
        if group == gd - 1:
            for other in range(gd):
                first = (X_TILES + 1 + other) * rows + EXTRA
                out[first : first + rows, :] = conv_tile_of(
                    scratch, rim_ref, bc_ref, tb_ref, sb_ref, 1,
                    (partner(me, slot) * gd + other) * STATE_DIM,
                )


def gate_kernel(z_ref, out_ref):
    tp, _, width = out_ref.shape
    for place in range(tp):
        out_ref[place] = z_ref[:, place * width : (place + 1) * width]


def state_kernel(group, tp, spans, bias_ref, log_ref, *rest):
    pieces = rest[:tp]
    conv_ref, scaled_ref, b_ref, grow_ref, mid_ref, prior_ref, ship_ref = rest[tp : tp + 7]
    ahead_ref = rest[tp + 7] if spans > 1 else None
    step_scr = rest[-1]
    rows = conv_ref.shape[0] // tp
    per_span = tp // spans
    me = lax.axis_index("tp")
    for slot in range(tp):
        place = partner(me, slot)
        at = pl.ds(pl.multiple_of(place * rows, rows), rows)
        for tile in range(X_TILES):
            conv_ref[at, tile * LANES : (tile + 1) * LANES] = pieces[slot][
                tile * rows : (tile + 1) * rows, :
            ]
        b_ref[at, :] = pieces[slot][X_TILES * rows : (X_TILES + 1) * rows, :]
        first = (X_TILES + 1) * rows
        step_scr[place] = pieces[slot][first : first + EXTRA, :].astype(F32)[:PER_GROUP]
    bias = column_of(bias_ref, group * PER_GROUP, rows)
    rate = jnp.exp(column_of(log_ref, group * PER_GROUP, rows))
    steps, logs = [], []
    for place in range(tp):
        raw = step_scr[place] + bias
        step = jnp.maximum(raw, 0.0) + jnp.log1p(jnp.exp(-jnp.abs(raw)))
        steps.append(step)
        logs.append(-step * rate)
    tri_r = lax.broadcasted_iota(jnp.int32, (rows, rows), 0)
    tri_c = lax.broadcasted_iota(jnp.int32, (rows, rows), 1)
    tri = jnp.where(tri_r <= tri_c, 1.0, 0.0).astype(BF16)
    parts = jnp.dot(in_three(jnp.concatenate(logs, axis=0)), tri, preferred_element_type=F32)
    count = tp * PER_GROUP
    sums = parts[:count] + parts[count : 2 * count] + parts[2 * count : 3 * count]
    columns = head_columns()
    prior = jnp.zeros((PER_GROUP, rows), F32)
    total = None
    for span in range(spans):
        inside, running = [], jnp.zeros((PER_GROUP, rows), F32)
        for piece in range(per_span):
            first = (span * per_span + piece) * PER_GROUP
            local = sums[first : first + PER_GROUP]
            inside.append(running + local)
            running = running + jnp.broadcast_to(local[:, rows - 1 :], (PER_GROUP, rows))
            if piece == max(per_span // 2 - 1, 0):
                middle = running
        for piece in range(per_span):
            place = span * per_span + piece
            grow_ref[place] = jnp.exp(inside[piece] - middle)
            scale = spread(jnp.exp(middle - inside[piece]) * steps[place], columns)
            at = slice(place * rows, (place + 1) * rows)
            scaled_ref[at, :] = (conv_ref[at, :].astype(F32) * scale).astype(BF16)
        at = slice(span * per_span * rows, (span + 1) * per_span * rows)
        summed = lax.dot_general(
            scaled_ref[at, :], b_ref[at, :], (((0,), (0,)), ((), ())), preferred_element_type=F32
        )
        summed = summed * spread_rows(jnp.exp(running - middle), columns)
        mid_ref[span] = middle
        prior_ref[span] = prior
        if spans > 1:
            ahead_ref[span] = total if total is not None else jnp.zeros_like(summed)
        total = summed if total is None else total * spread_rows(jnp.exp(running), columns) + summed
        prior = prior + running
    ship_ref[:GROUP_WIDTH, :] = total.astype(BF16)
    decay = jnp.exp(prior)
    high = decay.astype(BF16).astype(F32)
    ship_ref[GROUP_WIDTH:, :] = jnp.concatenate([high, decay - high], axis=0).astype(BF16)


def shipped(ref):
    rows = ref[GROUP_WIDTH:, :].astype(F32)
    return ref[:GROUP_WIDTH, :].astype(F32), rows[:PER_GROUP] + rows[PER_GROUP:]


def mix_kernel(gd, spans, tp, skip_ref, gate_ref, *rest):
    pieces, rest = rest[:tp], rest[tp:]
    held, outs = rest[: 4 * gd], rest[4 * gd :]
    rows = outs[0].shape[0] // tp
    per_span = tp // spans
    join = 2 if per_span % 2 == 0 else 1
    me = lax.axis_index("tp")
    columns = head_columns()
    for group in range(gd):
        conv_ref, scaled_ref, b_ref, grow_ref = held[4 * group : 4 * group + 4]
        c_ref, plain_ref, slope_ref = outs[3 * group : 3 * group + 3]
        first = (X_TILES + 1 + group) * rows + EXTRA
        for slot in range(tp):
            at = pl.ds(pl.multiple_of(partner(me, slot) * rows, rows), rows)
            c_ref[at, :] = pieces[slot][first : first + rows, :]
        skip = spread(column_of(skip_ref, group * PER_GROUP), columns)[:1]
        for place in range(0, tp, join):
            span = place // per_span
            at = slice(place * rows, (place + join) * rows)
            inside = slice(span * per_span * rows, (place + join) * rows)
            scores = lax.dot_general(
                c_ref[at, :], b_ref[inside, :], (((1,), (1,)), ((), ())),
                preferred_element_type=F32,
            )
            t_at = lax.broadcasted_iota(jnp.int32, scores.shape, 0)
            s_at = lax.broadcasted_iota(jnp.int32, scores.shape, 1) - (at.start - inside.start)
            masked = jnp.where(s_at <= t_at, scores, 0.0).astype(BF16)
            mixed = jnp.dot(masked, scaled_ref[inside, :], preferred_element_type=F32)
            grow = jnp.concatenate(
                [spread(grow_ref[other], columns) for other in range(place, place + join)], axis=0
            )
            mixed = mixed * grow + skip * conv_ref[at, :].astype(F32)
            z_at = group * GROUP_WIDTH
            gate = gate_ref[place : place + join, :, z_at : z_at + GROUP_WIDTH]
            gate = gate.reshape(join * rows, GROUP_WIDTH).astype(F32)
            gate = gate / (1.0 + jnp.exp(-gate))
            plain_ref[at, :] = mixed * gate
            slope_ref[at, :] = grow * gate


def out_kernel(spans, states, gain_ref, c_ref, plain_ref, slope_ref, *rest):
    mid_ref, prior_ref = rest[:2]
    rest = rest[2:]
    ahead_ref = None
    if spans > 1:
        ahead_ref, rest = rest[0], rest[1:]
    sent, rest = rest[:states], rest[states:]
    out_ref = rest[-1]
    columns = head_columns()
    ctx = lax.axis_index("ctx")
    state = None
    for steps in range(states, 0, -1):
        value, decay = shipped(sent[steps - 1])
        value = jnp.where(ctx >= steps, value, 0.0)
        state = value if state is None else state * spread_rows(decay, columns) + value
    span_rows = c_ref.shape[0] // spans
    tall = min(span_rows, 256)
    for span in range(spans):
        start = state
        if spans > 1:
            start = start * spread_rows(jnp.exp(prior_ref[span]), columns) + ahead_ref[span]
        start = (start * spread_rows(jnp.exp(mid_ref[span]), columns)).astype(BF16)
        for first in range(span * span_rows, (span + 1) * span_rows, tall):
            at = slice(first, first + tall)
            carried = lax.dot_general(
                c_ref[at, :], start, (((1,), (1,)), ((), ())), preferred_element_type=F32
            )
            gated = plain_ref[at, :] + carried * slope_ref[at, :]
            square = jnp.mean(gated * gated, axis=-1, keepdims=True)
            out_ref[at, :] = (gated * lax.rsqrt(square + 1e-5) * gain_ref[...]).astype(BF16)


def close(value):
    return pltpu.with_memory_space_constraint(value, pltpu.VMEM)


def far(value):
    return pltpu.with_memory_space_constraint(value, pltpu.HBM)


def vmem(count):
    return [pl.BlockSpec(memory_space=pltpu.VMEM)] * count


def smem(count):
    return [pl.BlockSpec(memory_space=pltpu.SMEM)] * count


def call(kernel, ins, outs, scratch, scalars=0, near=(), name=None):
    ins = [close(value) if place in near else value for place, value in enumerate(ins)]
    outs = [pltpu.VMEM(out.shape, out.dtype) for out in outs]
    return pl.pallas_call(
        kernel,
        in_specs=smem(scalars) + vmem(len(ins) - scalars),
        out_specs=vmem(len(outs)),
        out_shape=outs,
        scratch_shapes=scratch,
        compiler_params=pltpu.CompilerParams(vmem_limit_bytes=ROOM),
        cost_estimate=COSTS.get(name, LONG),
        name=name,
    )(*ins)


def joined(ship):
    rows = ship[GROUP_WIDTH:].astype(F32)
    return rows[:PER_GROUP] + rows[PER_GROUP:]


def packed(state, decay):
    high = decay.astype(BF16).astype(F32)
    return jnp.concatenate([state, high, decay - high], axis=0).astype(BF16)


def scanned(ship):
    count = lax.axis_size("ctx")
    if count <= 4:
        return [
            lax.ppermute(ship, "ctx", [(i, (i + steps) % count) for i in range(count)])
            for steps in range(1, count)
        ]
    state, decay = ship[:GROUP_WIDTH].astype(F32), joined(ship)
    steps = 1
    while steps < count:
        other = from_behind(packed(state, decay), "ctx", steps)
        scale = jnp.repeat(decay, HEAD_DIM, axis=0)
        state = other[:GROUP_WIDTH].astype(F32) * scale + state
        decay = decay * joined(other)
        steps *= 2
    return [from_behind(packed(state, decay), "ctx", 1)]


def shards(
    x_input, bc_input, z_input, dt_input, x_kernel, x_bias, bc_kernel, bc_bias, dt_bias, a_log,
    d_skip, norm_gain,
):
    tp = lax.axis_size("tp")
    rows = x_input.shape[0]
    ctx_rows = rows * tp
    gd = GROUPS // tp
    spans = max(1, ctx_rows // SPAN)
    width = gd * GROUP_WIDTH
    shape = jax.ShapeDtypeStruct

    def trade(parts):
        return [parts[0]] + [swap(close(parts[slot]), slot) for slot in range(1, tp)]

    count = bc_input.shape[2]
    every = x_input.shape[1] + 2 * count
    tail = pl.pallas_call(
        rim_kernel,
        grid=(1,),
        in_specs=[
            pl.BlockSpec((16, x_input.shape[1]), lambda i: (rows // 16 - 1, 0)),
            pl.BlockSpec((8, 2, count), lambda i: (rows // 8 - 1, 0, 0)),
        ],
        out_specs=pl.BlockSpec((RIM, every), lambda i: (0, 0)),
        out_shape=shape((RIM, every), BF16),
        compiler_params=pltpu.CompilerParams(vmem_limit_bytes=ROOM),
        name="rim",
    )(far(x_input), far(bc_input))
    rim = from_behind(tail, ("ctx", "tp"), 1)
    used = [
        far(value)
        for value in (
            x_input, bc_input, dt_input.T, x_kernel, x_bias.reshape(1, -1), bc_kernel, bc_bias
        )
    ]
    x_near, bc_near, *others = pl.pallas_call(
        functools.partial(load_kernel, len(used)),
        in_specs=[pl.BlockSpec(memory_space=pltpu.HBM)] * len(used),
        out_specs=vmem(len(used)),
        out_shape=[pltpu.VMEM(value.shape, value.dtype) for value in used],
        scratch_shapes=[pltpu.SemaphoreType.DMA((len(used),))],
        compiler_params=pltpu.CompilerParams(vmem_limit_bytes=ROOM),
        cost_estimate=LONG,
        name="load",
    )(*used)
    conv_scratch = pltpu.VMEM((8 + rows, LANES), F32)
    traded = []
    for group in range(gd):
        tall = (X_TILES + 1 + (gd if group == gd - 1 else 0)) * rows + EXTRA
        parts = call(
            functools.partial(send_kernel, group, tp, gd),
            [x_near, bc_near, others[0], rim] + others[1:],
            [shape((tall, LANES), BF16)] * tp,
            [conv_scratch, pltpu.VMEM((HEADS, rows), F32)],
            near=range(8),
            name=f"send{group}",
        )
        rim, parts, z_input = lax.optimization_barrier((rim, parts, z_input))
        traded.append(trade(parts))
        if group == 0:
            gates = call(
                gate_kernel, [z_input], [shape((tp, rows, width), BF16)], [], name="gates"
            )[0]
    gates, traded[0][tp // 2] = lax.optimization_barrier((gates, traded[0][tp // 2]))
    held = []
    for group in range(gd):
        outs = [
            shape((ctx_rows, GROUP_WIDTH), BF16),
            shape((ctx_rows, GROUP_WIDTH), BF16),
            shape((ctx_rows, STATE_DIM), BF16),
            shape((tp, PER_GROUP, rows), F32),
            shape((spans, PER_GROUP, rows), F32),
            shape((spans, PER_GROUP, rows), F32),
            shape((GROUP_WIDTH + 2 * PER_GROUP, STATE_DIM), BF16),
        ]
        if spans > 1:
            outs.append(shape((spans, GROUP_WIDTH, STATE_DIM), F32))
        made = call(
            functools.partial(state_kernel, group, tp, spans),
            [far(dt_bias), far(a_log)] + traded[group],
            outs,
            [pltpu.VMEM((tp, PER_GROUP, rows), F32)],
            scalars=2,
            near=range(2, 2 + tp),
            name=f"state{group}",
        )
        ship = made[6]
        kept_values = list(made[:6]) + list(made[7:])
        held.append((kept_values, scanned(ship)))
    gates = lax.all_to_all(gates, "tp", split_axis=0, concat_axis=0, tiled=True)
    if gd > 1:
        first = held[0][1]
        gates, first[0] = lax.optimization_barrier((gates, first[0]))
    gain = far(norm_gain.reshape(1, -1))
    ins = [far(d_skip), gates] + traded[-1]
    for values, _ in held:
        ins += values[:4]
    mixed = call(
        functools.partial(mix_kernel, gd, spans, tp),
        ins,
        ([shape((ctx_rows, STATE_DIM), BF16)] + [shape((ctx_rows, GROUP_WIDTH), F32)] * 2) * gd,
        [],
        scalars=1,
        near=range(1, len(ins)),
        name="mix",
    )
    out = None
    for group in range(gd):
        values, sent = held[group]
        ins = list(mixed[3 * group : 3 * group + 3]) + values[4:] + sent
        ins = [gain] + [close(value) for value in ins]
        aliases = {}
        specs = [pl.BlockSpec((1, GROUP_WIDTH), lambda i, g=group: (0, g))]
        specs += vmem(len(ins) - 1)
        if group > 0:
            aliases = {len(ins): 0}
            ins.append(out)
            specs.append(pl.BlockSpec(memory_space=pl.ANY))
        out = pl.pallas_call(
            functools.partial(out_kernel, spans, len(sent)),
            grid=(1,),
            in_specs=specs,
            out_specs=pl.BlockSpec((ctx_rows, GROUP_WIDTH), lambda i, g=group: (0, g)),
            out_shape=shape((ctx_rows, width), BF16),
            input_output_aliases=aliases,
            compiler_params=pltpu.CompilerParams(vmem_limit_bytes=ROOM),
            cost_estimate=LONG,
            name=f"out{group}",
        )(*ins)
    return out


def solution(mesh):
    lead = ("groups", "ctx", "tp")
    in_specs = (
        P(lead, None), P(lead, None, None), P(lead, None), P(lead, None), P(), P(), P(), P(),
        P("tp"), P("tp"), P("tp"), P("tp"),
    )
    out_specs = P(("groups", "ctx"), "tp")
    return jax.shard_map(shards, mesh=mesh, in_specs=in_specs, out_specs=out_specs, check_vma=False)
```
